32 devices in a mesh: pipe: 4 (over x, core), tensor: 8 (over z, y).
Axes of the slice: x: 2, y: 2, z: 4, core: 2. Of those that a mesh axis runs over, the one named last changes fastest.
Arguments:
- x_in: bfloat16 [4, 64, 7168], P(None, None, 'tensor'), may hold values from -6 to 6
- cotangent: bfloat16 [4, 64, 7168], P(None, None, 'tensor'), may hold values from -6 to 6
- w_in: bfloat16 [4, 4, 896, 28672], P('pipe', None, None, 'tensor'), may hold values from -0.09375 to 0.09375
- w_out: bfloat16 [4, 4, 3584, 7168], P('pipe', None, None, 'tensor'), may hold values from -0.046875 to 0.046875
Outputs:
- grad_acts: bfloat16 [4, 4, 64, 7168], P('pipe', None, None, 'tensor')
- grad_w_in: bfloat16 [4, 4, 896, 28672], P('pipe', None, None, 'tensor')
- grad_w_out: bfloat16 [4, 4, 3584, 7168], P('pipe', None, None, 'tensor')
The draws below stay inside these ranges and needn't reach their ends.
All inputs are finite; a program needn't handle non-finite values.
Results may differ from the reference program's by a relative error of at most 0.04.
Values may be sent and summed in bfloat16 or wider, within the bound.
A program may use at most 192 MiB of HBM per device.

```python
import jax
import jax.numpy as jnp
from jax import lax

D = 7168
FF = 28672
TOK = 64
MB = 4
LEVELS = 3
D_SLAB = 896
H_SLAB = 3584
N_PIPE = 4
N_TENSOR = 8


def levels(own_key, dims, split, smallest, high):
    def one(axis_at, parts):
        steps = jax.random.uniform(jax.random.fold_in(jax.random.fold_in(own_key, 6), axis_at), (parts,), jnp.float32, smallest / len(split), high / len(split))
        return jnp.repeat(jnp.exp(steps), dims[axis_at] // parts).reshape((-1,) + (1,) * (len(dims) - axis_at - 1))

    level = one(*split[0])
    for cut in split[1:]:
        level = level * one(*cut)
    return level


def bell_draw(key, shape, spread, bound, shards=(), kind=jnp.bfloat16):
    values = spread * jax.random.normal(key, shape, jnp.float32)
    if shards:
        values = values * levels(key, shape, shards, -0.22, 0.18)
    return jnp.clip(values, -bound, bound).astype(kind)


def setup_inputs(seed: int = 0) -> dict:
    splits = jax.random.split(jax.random.key(seed), 5)
    x_in = bell_draw(splits[0], (MB, TOK, D), 1.0, 6.0, ((2, 8),))
    cotangent = bell_draw(splits[1], (MB, TOK, D), 1.0, 6.0, ((2, 8),))
    w_in = bell_draw(splits[2], (N_PIPE, LEVELS + 1, D_SLAB, FF), ((LEVELS + 1) * D_SLAB) ** -0.5, 0.09375, ((0, 4), (3, 8)))
    w_out = bell_draw(splits[3], (N_PIPE, LEVELS + 1, H_SLAB, D), ((LEVELS + 1) * H_SLAB) ** -0.5, 0.046875, ((0, 4), (3, 8)))
    return dict(x_in=x_in, cotangent=cotangent, w_in=w_in, w_out=w_out)


def gelu_value(values):
    return jax.nn.gelu(values, approximate=True)

def gelu_slope(preact):
    result, pullback = jax.vjp(gelu_value, preact)
    return pullback(jnp.ones_like(preact))[0]

def rounded(values):
    return lax.optimization_barrier(values.astype(jnp.bfloat16)).astype(jnp.float32)

def to_slabs(array, slab_width):
    return array.astype(jnp.float32).reshape(MB, TOK, N_TENSOR, slab_width).transpose(0, 2, 1, 3)

def from_slabs(array):
    return array.transpose(0, 2, 1, 3).reshape(MB, TOK, N_TENSOR * array.shape[3])

def reference(x_in, cotangent, w_in, w_out):
    n_terms = LEVELS + 1
    slab_ids = jnp.arange(N_TENSOR, dtype=jnp.int32)
    partner = [slab_ids] + [jnp.bitwise_xor(slab_ids, jnp.int32(1 << level)) for level in range(LEVELS)]

    def blocks(layer_no):
        w_first = w_in[layer_no].astype(jnp.float32).reshape(n_terms, D_SLAB, N_TENSOR, H_SLAB).transpose(0, 2, 1, 3)
        w_second = w_out[layer_no].astype(jnp.float32).reshape(n_terms, H_SLAB, N_TENSOR, D_SLAB).transpose(0, 2, 1, 3)
        return (w_first, w_second)
    activity = to_slabs(x_in, D_SLAB)
    stored = []
    for layer_no in range(N_PIPE):
        w_first, w_second = blocks(layer_no)
        preact = sum((jnp.einsum('mntd,ndf->mntf', activity[:, partner[term]], w_first[term]) for term in range(n_terms)))
        hidden = rounded(gelu_value(preact))
        layer_out = activity + sum((jnp.einsum('mntf,nfd->mntd', hidden[:, partner[term]], w_second[term]) for term in range(n_terms)))
        stored.append((activity, preact, hidden))
        activity = rounded(layer_out)
    gradient = to_slabs(cotangent, D_SLAB)
    grad_list = [None] * N_PIPE
    first_list = [None] * N_PIPE
    second_list = [None] * N_PIPE
    for layer_no in reversed(range(N_PIPE)):
        activity, preact, hidden = stored[layer_no]
        w_first, w_second = blocks(layer_no)
        hid_grad = sum((rounded(jnp.einsum('mntd,nfd->mntf', gradient, w_second[term]))[:, partner[term]] for term in range(n_terms)))
        dpre = rounded(hid_grad * gelu_slope(preact))
        input_grad = gradient + sum((rounded(jnp.einsum('mntf,ndf->mntd', dpre, w_first[term]))[:, partner[term]] for term in range(n_terms)))
        first_terms = []
        second_terms = []
        for term in range(n_terms):
            g_first = jnp.einsum('mntd,mntf->ndf', activity[:, partner[term]], dpre)
            first_terms.append(g_first.transpose(1, 0, 2).reshape(D_SLAB, FF))
            g_second = jnp.einsum('mntf,mntd->nfd', hidden[:, partner[term]], gradient)
            second_terms.append(g_second.transpose(1, 0, 2).reshape(H_SLAB, D))
        first_list[layer_no] = jnp.stack(first_terms).astype(jnp.bfloat16)
        second_list[layer_no] = jnp.stack(second_terms).astype(jnp.bfloat16)
        grad_list[layer_no] = from_slabs(input_grad).astype(jnp.bfloat16)
        gradient = rounded(input_grad)
    return (jnp.stack(grad_list), jnp.stack(first_list), jnp.stack(second_list))
```

```python
import jax
import jax.numpy as jnp
from jax import lax
from jax.sharding import PartitionSpec as P

CHUNKS = 2
AXES = ("pipe", "tensor")


def gelu_value(values):
    return jax.nn.gelu(values, approximate=True)


def gelu_slope(preact):
    result, pullback = jax.vjp(gelu_value, preact)
    return pullback(jnp.ones_like(preact))[0]


def move(value, source, target, flip):
    width = lax.axis_size("tensor")
    route = [(source * width + i, target * width + (i ^ flip)) for i in range(width)]
    return lax.ppermute(value, AXES, route)


def times(lhs, rhs, contract):
    return lax.dot_general(lhs, rhs, (contract, ((), ())), preferred_element_type=jnp.float32)


def body(x_in, cotangent, w_in, w_out):
    levels = lax.axis_size("tensor").bit_length() - 1
    sections = lax.axis_size("pipe")
    my_section = lax.axis_index("pipe")
    batches, tok_rows, in_slab = x_in.shape
    w_first = w_in[0]
    w_second = w_out[0]
    hid_slab = w_first.shape[2]
    n_terms = levels + 1
    flips = [0] + [1 << level for level in range(levels)]
    rows = batches * tok_rows // CHUNKS
    split = lambda array: list(array.reshape(CHUNKS, rows, in_slab))
    chunks = range(CHUNKS)

    table = lambda: [[None] * CHUNKS for _ in range(sections + 1)]
    near, hid_near, preacts = table(), table(), table()
    gradients, dpres, input_grads = table(), table(), table()
    kept_values = sections * batches * tok_rows * (n_terms * (in_slab + hid_slab) + 2 * hid_slab)
    hold = kept_values > 2 * (w_first.size + w_second.size)

    def keep(store, layer, c):
        if not hold:
            return
        old, new = store[sections][c], store[layer][c]
        if old is not None:
            new = jax.tree.map(lambda n, o: jnp.where(my_section == layer, n, o), new, old)
        store[sections][c] = new

    starts = split(x_in)
    outs = [None] * CHUNKS
    for layer in range(sections):
        for c in chunks:
            if layer == 0:
                terms = [starts[c]] + [move(starts[c], 0, 0, flip) for flip in flips[1:]]
            else:
                terms = [move(outs[c], layer - 1, layer, flip) for flip in flips]
            near[layer][c] = terms
        for c in chunks:
            stacked = jnp.stack(near[layer][c])
            preact = jnp.einsum(
                "ktd,kdf->tf", stacked, w_first, preferred_element_type=jnp.float32
            )
            hidden = gelu_value(preact).astype(jnp.bfloat16)
            preacts[layer][c] = preact
            hid_near[layer][c] = [hidden] + [move(hidden, layer, layer, flip) for flip in flips[1:]]
            keep(near, layer, c)
            keep(hid_near, layer, c)
            keep(preacts, layer, c)
        if layer == sections - 1:
            continue
        for c in chunks:
            total = near[layer][c][0].astype(jnp.float32)
            for k in range(n_terms):
                total = total + times(hid_near[layer][c][k], w_second[k], ((1,), (0,)))
            outs[c] = total.astype(jnp.bfloat16)

    gradients[sections - 1] = split(cotangent)
    for layer in reversed(range(sections)):
        if layer < sections - 1:
            gradients[layer] = [move(input_grads[layer + 1][c], layer + 1, layer, 0) for c in chunks]
        pieces = [None] * CHUNKS
        for c in chunks:
            sent = []
            for k in reversed(range(1, n_terms)):
                piece = times(gradients[layer][c], w_second[k], ((1,), (1,))).astype(jnp.bfloat16)
                sent.append(move(piece, layer, layer, flips[k]))
            own = times(gradients[layer][c], w_second[0], ((1,), (1,))).astype(jnp.bfloat16)
            pieces[c] = [own] + sent
        for c in chunks:
            hid_grad = sum(piece.astype(jnp.float32) for piece in pieces[c])
            preact = preacts[sections if hold else layer][c]
            dpre = (hid_grad * gelu_slope(preact)).astype(jnp.bfloat16)
            dpres[layer][c] = dpre
            keep(gradients, layer, c)
            keep(dpres, layer, c)
            sent = []
            for k in reversed(range(1, n_terms)):
                piece = times(dpre, w_first[k], ((1,), (1,))).astype(jnp.bfloat16)
                sent.append(move(piece, layer, layer, flips[k]))
            own = times(dpre, w_first[0], ((1,), (1,))).astype(jnp.bfloat16)
            total = gradients[layer][c].astype(jnp.float32)
            for piece in [own] + sent:
                total = total + piece.astype(jnp.float32)
            input_grads[layer][c] = total.astype(jnp.bfloat16)
            keep(input_grads, layer, c)

    def join(parts):
        return jnp.stack([jnp.concatenate([part[k] for part in parts]) for k in range(n_terms)])

    def pick(make):
        if hold:
            return make(sections)
        return lax.switch(my_section, [lambda layer=layer: make(layer) for layer in range(sections)])

    hid_all, grad_all = pick(lambda at: (join(hid_near[at]), jnp.concatenate(gradients[at])))
    grad_second = jnp.einsum(
        "ktf,td->kfd", hid_all, grad_all, preferred_element_type=jnp.float32
    ).astype(jnp.bfloat16)
    near_all, dpre_all = pick(lambda at: (join(near[at]), jnp.concatenate(dpres[at])))
    grad_first = jnp.einsum(
        "ktd,tf->kdf", near_all, dpre_all, preferred_element_type=jnp.float32
    ).astype(jnp.bfloat16)
    if hold:
        mine = jnp.concatenate(input_grads[sections])
        return (mine.reshape(1, batches, tok_rows, in_slab), grad_first[None], grad_second[None])
    mine = jnp.concatenate(input_grads[0])
    for layer in range(1, sections):
        mine = jnp.where(my_section == layer, jnp.concatenate(input_grads[layer]), mine)
    return (mine.reshape(1, batches, tok_rows, in_slab), grad_first[None], grad_second[None])


def solution(mesh):
    placed = (
        P(None, None, "tensor"),
        P(None, None, "tensor"),
        P("pipe", None, None, "tensor"),
        P("pipe", None, None, "tensor"),
    )
    return jax.shard_map(
        body,
        mesh=mesh,
        in_specs=placed,
        out_specs=(
            P("pipe", None, None, "tensor"),
            P("pipe", None, None, "tensor"),
            P("pipe", None, None, "tensor"),
        ),
        check_vma=False,
    )
```

```python
import jax
import jax.numpy as jnp
from jax import lax
from jax.sharding import PartitionSpec as P

CHUNKS = 1
AXES = ("pipe", "tensor")


def gelu_value(values):
    return jax.nn.gelu(values, approximate=True)


def gelu_slope(preact):
    result, pullback = jax.vjp(gelu_value, preact)
    return pullback(jnp.ones_like(preact))[0]


def move(value, source, target, flip):
    width = lax.axis_size("tensor")
    route = [(source * width + i, target * width + (i ^ flip)) for i in range(width)]
    return lax.ppermute(value, AXES, route)


def times(lhs, rhs, contract):
    return lax.dot_general(lhs, rhs, (contract, ((), ())), preferred_element_type=jnp.float32)


def body(x_in, cotangent, w_in, w_out):
    levels = lax.axis_size("tensor").bit_length() - 1
    sections = lax.axis_size("pipe")
    my_section = lax.axis_index("pipe")
    batches, tok_rows, in_slab = x_in.shape
    w_first = w_in[0]
    w_second = w_out[0]
    hid_slab = w_first.shape[2]
    n_terms = levels + 1
    flips = [0] + [1 << level for level in range(levels)]
    rows = batches * tok_rows // CHUNKS
    split = lambda array: list(array.reshape(CHUNKS, rows, in_slab))
    chunks = range(CHUNKS)

    table = lambda: [[None] * CHUNKS for _ in range(sections + 1)]
    near, hid_near, preacts = table(), table(), table()
    gradients, dpres, input_grads = table(), table(), table()
    kept_values = sections * batches * tok_rows * (n_terms * (in_slab + hid_slab) + 2 * hid_slab)
    hold = kept_values > 2 * (w_first.size + w_second.size)

    def keep(store, layer, c):
        if not hold:
            return
        old, new = store[sections][c], store[layer][c]
        if old is not None:
            new = jax.tree.map(lambda n, o: jnp.where(my_section == layer, n, o), new, old)
        store[sections][c] = new

    starts = split(x_in)
    outs = [None] * CHUNKS
    for layer in range(sections):
        for c in chunks:
            if layer == 0:
                terms = [starts[c]] + [move(starts[c], 0, 0, flip) for flip in flips[1:]]
            else:
                terms = [move(outs[c], layer - 1, layer, flip) for flip in flips]
            near[layer][c] = terms
        for c in chunks:
            stacked = jnp.stack(near[layer][c])
            preact = jnp.einsum(
                "ktd,kdf->tf", stacked, w_first, preferred_element_type=jnp.float32
            )
            hidden = gelu_value(preact).astype(jnp.bfloat16)
            preacts[layer][c] = preact
            hid_near[layer][c] = [hidden] + [move(hidden, layer, layer, flip) for flip in flips[1:]]
            keep(near, layer, c)
            keep(hid_near, layer, c)
            keep(preacts, layer, c)
        if layer == sections - 1:
            continue
        for c in chunks:
            total = near[layer][c][0].astype(jnp.float32)
            for k in range(n_terms):
                total = total + times(hid_near[layer][c][k], w_second[k], ((1,), (0,)))
            outs[c] = total.astype(jnp.bfloat16)

    gradients[sections - 1] = split(cotangent)
    for layer in reversed(range(sections)):
        if layer < sections - 1:
            gradients[layer] = [move(input_grads[layer + 1][c], layer + 1, layer, 0) for c in chunks]
        pieces = [None] * CHUNKS
        for c in chunks:
            sent = []
            for k in reversed(range(1, n_terms)):
                piece = times(gradients[layer][c], w_second[k], ((1,), (1,))).astype(jnp.bfloat16)
                sent.append(move(piece, layer, layer, flips[k]))
            own = times(gradients[layer][c], w_second[0], ((1,), (1,))).astype(jnp.bfloat16)
            pieces[c] = [own] + sent
        for c in chunks:
            hid_grad = sum(piece.astype(jnp.float32) for piece in pieces[c])
            preact = preacts[sections if hold else layer][c]
            dpre = (hid_grad * gelu_slope(preact)).astype(jnp.bfloat16)
            dpres[layer][c] = dpre
            keep(gradients, layer, c)
            keep(dpres, layer, c)
            sent = []
            for k in reversed(range(1, n_terms)):
                piece = times(dpre, w_first[k], ((1,), (1,))).astype(jnp.bfloat16)
                sent.append(move(piece, layer, layer, flips[k]))
            own = times(dpre, w_first[0], ((1,), (1,))).astype(jnp.bfloat16)
            total = gradients[layer][c].astype(jnp.float32)
            for piece in [own] + sent:
                total = total + piece.astype(jnp.float32)
            input_grads[layer][c] = total.astype(jnp.bfloat16)
            keep(input_grads, layer, c)

    def join(parts):
        return jnp.stack([jnp.concatenate([part[k] for part in parts]) for k in range(n_terms)])

    def pick(make):
        if hold:
            return make(sections)
        return lax.switch(my_section, [lambda layer=layer: make(layer) for layer in range(sections)])

    hid_all, grad_all = pick(lambda at: (join(hid_near[at]), jnp.concatenate(gradients[at])))
    grad_second = jnp.einsum(
        "ktf,td->kfd", hid_all, grad_all, preferred_element_type=jnp.float32
    ).astype(jnp.bfloat16)
    near_all, dpre_all = pick(lambda at: (join(near[at]), jnp.concatenate(dpres[at])))
    grad_first = jnp.einsum(
        "ktd,tf->kdf", near_all, dpre_all, preferred_element_type=jnp.float32
    ).astype(jnp.bfloat16)
    if hold:
        mine = jnp.concatenate(input_grads[sections])
        return (mine.reshape(1, batches, tok_rows, in_slab), grad_first[None], grad_second[None])
    mine = jnp.concatenate(input_grads[0])
    for layer in range(1, sections):
        mine = jnp.where(my_section == layer, jnp.concatenate(input_grads[layer]), mine)
    return (mine.reshape(1, batches, tok_rows, in_slab), grad_first[None], grad_second[None])


def solution(mesh):
    placed = (
        P(None, None, "tensor"),
        P(None, None, "tensor"),
        P("pipe", None, None, "tensor"),
        P("pipe", None, None, "tensor"),
    )
    return jax.shard_map(
        body,
        mesh=mesh,
        in_specs=placed,
        out_specs=(
            P("pipe", None, None, "tensor"),
            P("pipe", None, None, "tensor"),
            P("pipe", None, None, "tensor"),
        ),
        check_vma=False,
    )
```
